256 devices in a mesh: row: 32 (over z, x_hi, core), col: 8 (over x_lo, y).
Axes of the slice: x: 4 (x_hi: 2, x_lo: 2; x = x_hi * 2 + x_lo), y: 4, z: 8, core: 2. Of those that a mesh axis runs over, the one named last changes fastest.
Arguments:
- a_blocks: bfloat16 [32, 8, 16, 128, 128], P('row', 'col'), may hold values from -6 to 6
- a_rows: int32 [32, 8, 16], P('row', 'col'), may hold values from 0 to 3
- b_blocks: bfloat16 [32, 8, 32, 128, 128], P('row', 'col'), may hold values from -0.25 to 0.25
- b_cols: int32 [32, 8, 32], P('row', 'col'), may hold values from 0 to 7
- pair_list: int32 [32, 8, 4, 2, 256], P('row', 'col'), may hold values from 0 to 31, as said below
- pair_count: int32 [32, 8, 4], P('row', 'col'), may hold values from 1 to 256, as said below
- row_order: int32 [32, 4], P('row'), may hold values from 0 to 3, each once within a row
Outputs:
- product_matrix: bfloat16 [16384, 8192], P('row', 'col')
The draws below stay inside these ranges and needn't reach their ends.
Inputs may be any that keep to these rules, and one draw needn't show every extreme that they name: pair_list[..., 0, :] names a left slot below 16 and pair_list[..., 1, :] a right slot below 32; no list of one device and stop names the same pair twice. `pair_count`: in every stop some device's list is full.
All inputs are finite; a program needn't handle non-finite values.
Results may differ from the reference program's by a relative error of at most 0.001.
Values may be sent and summed in bfloat16 or wider, within the bound.
A program may use at most 64 MiB of HBM per device.

```python
import jax
import jax.numpy as jnp
from jax import lax

BS = 128
CROWS = 4
CCOLS = 8
A_SLOTS = 16
B_SLOTS = 32
PAIRS = 256
STOPS = 4
N_ROW = 32
N_COL = 8


def draw_pair_list(key, part):
    keys = jax.random.split(key, N_ROW * N_COL * STOPS)

    def pick_pairs(one_key):
        first_key = jax.random.fold_in(one_key, 21)
        second_key = jax.random.fold_in(one_key, 22)
        others = jax.random.permutation(first_key, A_SLOTS * B_SLOTS - 2)[:PAIRS - 2] + 1
        ends = jnp.array([0, A_SLOTS * B_SLOTS - 1], dtype=jnp.int32)
        chosen = jnp.concatenate([ends, others.astype(jnp.int32)], axis=0)
        chosen = jax.random.permutation(second_key, chosen)
        return jnp.stack([chosen // B_SLOTS, chosen % B_SLOTS], axis=0)
    pair_table = jax.vmap(pick_pairs)(keys)
    return pair_table.reshape(N_ROW, N_COL, STOPS, 2, PAIRS).astype(jnp.int32)


def draw_pair_count(key, part):
    first_key = jax.random.fold_in(key, 11)
    second_key = jax.random.fold_in(key, 12)
    spread = jax.random.randint(first_key, (N_ROW, N_COL, STOPS), 0, PAIRS)
    counts = 1 + spread * spread // PAIRS
    busiest = jax.random.randint(second_key, (STOPS,), 0, N_ROW * N_COL)
    flat_index = jnp.arange(N_ROW * N_COL, dtype=jnp.int32).reshape(N_ROW, N_COL, 1)
    return jnp.where(flat_index == busiest[None, None, :], PAIRS, counts).astype(jnp.int32)


def place_ends(values, rng, least, top_value):
    shape = values.shape
    spot = [jax.random.randint(jax.random.fold_in(rng, axis), (), 0, shape[axis]) for axis in range(len(shape))]
    values = values.at[tuple(spot)].set(least)
    longest = shape.index(max(shape))
    spot[longest] = (spot[longest] + 1) % shape[longest]
    return values.at[tuple(spot)].set(top_value)


def levels(stream_key, shape, shards, smallest, high):
    gain, own = 1.0, jax.random.fold_in(stream_key, 6)
    for dim, shards_of in shards:
        heights = jnp.exp(jax.random.uniform(jax.random.fold_in(own, dim), (shards_of,), jnp.float32, smallest / len(shards), high / len(shards)))
        gain = gain * jnp.repeat(heights, shape[dim] // shards_of).reshape([-1 if axis == dim else 1 for axis in range(len(shape))])
    return gain


def noise(key, extent, scale, limit, cuts=(), kind=jnp.bfloat16):
    drawn = jax.random.normal(key, extent, jnp.float32) * scale
    if len(cuts) > 0:
        drawn = levels(key, extent, cuts, -0.22, 0.18) * drawn
    return jnp.clip(drawn, min=-limit, max=limit).astype(kind)


def setup_inputs(seed: int = 0) -> dict:
    streams_of = jax.random.split(jax.random.key(seed), 8)
    return {
        "a_blocks": noise(streams_of[0], (N_ROW, N_COL, A_SLOTS, BS, BS), 1.0, 6.0, ((0, 32), (1, 8))),
        "a_rows": place_ends(jax.random.randint(streams_of[1], (N_ROW, N_COL, A_SLOTS), 0, CROWS), jax.random.fold_in(streams_of[1], 1), 0, CROWS - 1).astype(jnp.int32),
        "b_blocks": noise(streams_of[2], (N_ROW, N_COL, B_SLOTS, BS, BS), (BS * 4) ** -0.5, 0.25, ((0, 32), (1, 8))),
        "b_cols": place_ends(jax.random.randint(streams_of[3], (N_ROW, N_COL, B_SLOTS), 0, CCOLS), jax.random.fold_in(streams_of[3], 1), 0, CCOLS - 1).astype(jnp.int32),
        "pair_list": draw_pair_list(jax.random.fold_in(streams_of[7], 71), 0),
        "pair_count": draw_pair_count(jax.random.fold_in(streams_of[7], 71), 0),
        "row_order": jax.vmap(lambda own: jax.random.permutation(own, CROWS))(jax.random.split(streams_of[6], N_ROW)).reshape((N_ROW, CROWS)).astype(jnp.int32),
    }


def reference(a_blocks, a_rows, b_blocks, b_cols, pair_list, pair_count, row_order):
    n_slots = CROWS * CCOLS

    def per_device(device):
        row_index = device // N_COL
        col_index = device % N_COL
        accum = jnp.zeros((n_slots, BS, BS), jnp.float32)
        for stop in range(STOPS):
            source_col = (col_index + row_index + stop) % N_COL
            source_row = (row_index + col_index + stop) % N_ROW
            left_set = a_blocks[row_index, source_col].astype(jnp.float32)
            left_ids = a_rows[row_index, source_col]
            right_set = b_blocks[source_row, col_index].astype(jnp.float32)
            right_ids = b_cols[source_row, col_index]
            pick = pair_list[row_index, col_index, stop]
            products = jnp.einsum("pij,pjk->pik", left_set[pick[0]], right_set[pick[1]])
            is_live = (jnp.arange(PAIRS, dtype=jnp.int32) < pair_count[row_index, col_index, stop]).astype(jnp.float32)
            target = row_order[row_index][left_ids[pick[0]]] * CCOLS + right_ids[pick[1]]
            accum = accum + jax.ops.segment_sum(products * is_live[:, None, None], target, n_slots)
        panel = accum.reshape(CROWS, CCOLS, BS, BS).transpose(0, 2, 1, 3).reshape(CROWS * BS, CCOLS * BS)
        return panel.astype(jnp.bfloat16)

    panels = lax.map(per_device, jnp.arange(N_ROW * N_COL, dtype=jnp.int32))
    panels = panels.reshape(N_ROW, N_COL, CROWS * BS, CCOLS * BS).transpose(0, 2, 1, 3)
    return panels.reshape(N_ROW * CROWS * BS, N_COL * CCOLS * BS)
```

```python
import functools

import jax
import jax.numpy as jnp
from jax import lax
from jax.experimental import pallas as pl
from jax.experimental.pallas import tpu as pltpu
from jax.sharding import PartitionSpec as P

CROWS = 4
CCOLS = 8
STOPS = 4
CHUNKS = 4
UNROLL = 8
MESH = pl.DeviceIdType.MESH
ANY = pl.BlockSpec(memory_space=pl.ANY)
SMEM = pl.BlockSpec(memory_space=pltpu.SMEM)


def gather_kernel(
    n_row, n_col, a, b, arow, bcol, ar, br, arr, bcr, a_ss, a_rs, b_ss, b_rs, m_ss, m_rs
):
    r = lax.axis_index("row")
    c = lax.axis_index("col")
    j = lax.rem(r, 4)
    step = b.shape[0] // CHUNKS

    def row(d):
        return lax.rem(r + d + n_row, n_row)

    def col(d):
        return lax.rem(c + d + 8 * n_col, n_col)

    bar = pltpu.get_barrier_semaphore()
    for s in range(STOPS):
        src = lax.rem(c + r + s, n_col)
        dst = lax.rem(c - r - s + 8 * n_col, n_col)

        @pl.when(src != c)
        def _():
            pl.semaphore_signal(bar, 1, device_id=(r, src), device_id_type=MESH)
            pl.semaphore_signal(bar, 1, device_id=(r, dst), device_id_type=MESH)

    for s in range(STOPS + 3):
        pass

    def greet(d):
        pl.semaphore_signal(bar, 1, device_id=(row(d), c), device_id_type=MESH)

    for s in range(STOPS):

        @pl.when(c + s != 0)
        def _():
            pl.semaphore_signal(
                bar, 1, device_id=(lax.rem(r + c + s, n_row), c), device_id_type=MESH
            )
            pl.semaphore_signal(
                bar, 1, device_id=(lax.rem(r - c - s + n_row, n_row), c), device_id_type=MESH
            )

    for d in (1, 2, 3):
        greet(d)
        greet(-d)
    has_self_a = lax.rem(r + STOPS - 1, n_col) < STOPS
    self_a = jnp.int32(0)
    for s in range(STOPS):
        self_a = self_a + jnp.where(lax.rem(r + s, n_col) == 0, 1, 0)
    self_b = jnp.where(c == 0, 1, 0)
    pl.semaphore_wait(bar, 2 * (STOPS - self_a) + 2 * (STOPS - self_b) + 6)

    def rc(src, dst, ss, rs, dev):
        return pltpu.make_async_remote_copy(
            src, dst, ss, rs, device_id=dev, device_id_type=MESH
        )

    def chunk(k):
        return pl.ds(k * step, step)

    for s in range(STOPS):
        dst = lax.rem(c - r - s + 8 * n_col, n_col)

        @pl.when(lax.rem(r + s, n_col) != 0)
        def _():
            rc(arow, arr.at[s], m_ss.at[s], m_rs.at[s], (r, dst)).start()

        @pl.when(c + s != 0)
        def _():
            rc(
                bcol, bcr.at[s], m_ss.at[4 + s], m_rs.at[4 + s],
                (lax.rem(r - c - s + n_row, n_row), c),
            ).start()

    @pl.when(c != 0)
    def _():
        for k in range(CHUNKS):
            rc(
                b.at[chunk(k)], br.at[0, chunk(k)], b_ss.at[0, k], b_rs.at[0, k],
                (lax.rem(r - c + n_row, n_row), c),
            ).start()

    for s in range(STOPS):
        dst = lax.rem(c - r - s + 8 * n_col, n_col)

        @pl.when(lax.rem(r + s, n_col) != 0)
        def _():
            rc(a, ar.at[s], a_ss.at[s], a_rs.at[s], (r, dst)).start()

    def wait_recv(w, k):
        rc(br.at[w, chunk(k)], br.at[w, chunk(k)], b_ss.at[0, k], b_rs.at[w, k], (r, c)).wait_recv()

    def send(src_w, k, w, d, slot, own):
        src = b.at[chunk(k)] if own else br.at[src_w, chunk(k)]
        return rc(src, br.at[w, chunk(k)], b_ss.at[slot, k], b_rs.at[w, k], (row(d), c))

    plans = {
        0: ((0, 3, -3),),
        1: ((0, 1, -1), (0, 2, -2), (1, 2, -1), (2, 3, -1), (3, 2, 1)),
        2: ((0, 1, -1), (0, 3, -3), (2, 1, 1)),
        3: ((0, 1, -1), (0, 2, -2), (2, 3, -1)),
    }

    def run(plan, own):
        for k in range(CHUNKS):
            seen = {0} if own else set()
            for slot, (src_w, w, d) in enumerate(plan):
                if src_w not in seen:
                    wait_recv(src_w, k)
                    seen.add(src_w)
                send(src_w, k, w, d, slot + 1, own and src_w == 0).start()
        for k in range(CHUNKS):
            seen = {0} | {p[0] for p in plan}
            for w in range(STOPS):
                if w not in seen or (w == 0 and not own and 0 not in {p[0] for p in plan}):
                    wait_recv(w, k)
            for slot, (src_w, w, d) in enumerate(plan):
                send(src_w, k, w, d, slot + 1, own and src_w == 0).wait_send()

    for jj in range(4):
        for own in (False, True):

            @pl.when((j == jj) & ((c == 0) if own else (c != 0)))
            def _():
                run(plans[jj], own)

    @pl.when(c != 0)
    def _():
        for k in range(CHUNKS):
            rc(b.at[chunk(k)], br.at[0, chunk(k)], b_ss.at[0, k], b_rs.at[0, k], (r, c)).wait_send()

    for s in range(STOPS):

        @pl.when(lax.rem(r + s, n_col) != 0)
        def _():
            rc(a, ar.at[s], a_ss.at[s], a_rs.at[s], (r, c)).wait()
            rc(arow, arr.at[s], m_ss.at[s], m_rs.at[s], (r, c)).wait()

        @pl.when(c + s != 0)
        def _():
            rc(bcol, bcr.at[s], m_ss.at[4 + s], m_rs.at[4 + s], (r, c)).wait()


def multiply_kernel(
    n_col, a, b, ar, br, arow, bcol, arr, bcr, pairs, count, order, out, avm, bvm, acc, a_sem, b_sem
):
    r = lax.axis_index("row")
    c = lax.axis_index("col")

    for s in range(STOPS):
        own_a = lax.rem(r + s, n_col) == 0

        @pl.when(own_a)
        def _():
            pltpu.make_async_copy(a, avm.at[s], a_sem.at[s]).start()

        @pl.when(jnp.logical_not(own_a))
        def _():
            pltpu.make_async_copy(ar.at[s], avm.at[s], a_sem.at[s]).start()

        if s == 0:

            @pl.when(c == 0)
            def _():
                pltpu.make_async_copy(b, bvm.at[s], b_sem.at[s]).start()

            @pl.when(c != 0)
            def _():
                pltpu.make_async_copy(br.at[s], bvm.at[s], b_sem.at[s]).start()
        else:
            pltpu.make_async_copy(br.at[s], bvm.at[s], b_sem.at[s]).start()

    acc[...] = jnp.zeros_like(acc)
    for s in range(STOPS):
        own_a = lax.rem(r + s, n_col) == 0
        own_b = c + s == 0
        pltpu.make_async_copy(ar.at[s], avm.at[s], a_sem.at[s]).wait()
        pltpu.make_async_copy(br.at[s], bvm.at[s], b_sem.at[s]).wait()
        live = count[0, 0, s]

        def body(t, carry):
            for u in range(UNROLL):
                p = t * UNROLL + u
                left = pairs[0, 0, s, 0, p]
                right = pairs[0, 0, s, 1, p]
                at_row = jnp.where(own_a, arow[0, 0, left], arr[s, 0, 0, left])
                at_col = jnp.where(own_b, bcol[0, 0, right], bcr[s, 0, 0, right])
                target = order[0, at_row] * CCOLS + at_col
                target = jnp.where(p < live, target, CROWS * CCOLS)
                acc[target] += jnp.dot(
                    avm[s, left], bvm[s, right], preferred_element_type=jnp.float32
                )
            return carry

        lax.fori_loop(0, (live + UNROLL - 1) // UNROLL, body, 0)
    edge = acc.shape[1]
    for i in range(CROWS):
        for k in range(CCOLS):
            out[i * edge : (i + 1) * edge, k * edge : (k + 1) * edge] = acc[
                i * CCOLS + k
            ].astype(out.dtype)


def per_device(n_row, n_col, a_blocks, a_rows, b_blocks, b_cols, pair_list, pair_count, row_order):
    a = a_blocks[0, 0]
    b = b_blocks[0, 0]
    n_a, edge, _ = a.shape
    n_b = b.shape[0]
    dt = a.dtype
    dma = pltpu.SemaphoreType.DMA
    ar, br, arr, bcr = pl.pallas_call(
        functools.partial(gather_kernel, n_row, n_col),
        out_shape=(
            jax.ShapeDtypeStruct((STOPS, n_a, edge, edge), dt),
            jax.ShapeDtypeStruct((STOPS, n_b, edge, edge), dt),
            jax.ShapeDtypeStruct((STOPS, 1, 1, n_a), jnp.int32),
            jax.ShapeDtypeStruct((STOPS, 1, 1, n_b), jnp.int32),
        ),
        in_specs=[ANY] * 4,
        out_specs=(ANY,) * 4,
        scratch_shapes=[
            dma((STOPS,)),
            dma((STOPS,)),
            dma((6, CHUNKS)),
            dma((STOPS, CHUNKS)),
            dma((2 * STOPS,)),
            dma((2 * STOPS,)),
        ],
        compiler_params=pltpu.CompilerParams(collective_id=0, has_side_effects=True),
        name="gather",
    )(a, b, a_rows, b_cols)
    return pl.pallas_call(
        functools.partial(multiply_kernel, n_col),
        out_shape=jax.ShapeDtypeStruct((CROWS * edge, CCOLS * edge), dt),
        in_specs=[ANY] * 4 + [SMEM] * 7,
        out_specs=pl.BlockSpec(memory_space=pltpu.VMEM),
        scratch_shapes=[
            pltpu.VMEM((STOPS, n_a, edge, edge), dt),
            pltpu.VMEM((STOPS, n_b, edge, edge), dt),
            pltpu.VMEM((CROWS * CCOLS + 1, edge, edge), jnp.float32),
            dma((STOPS,)),
            dma((STOPS,)),
        ],
        name="multiply",
    )(a, b, ar, br, a_rows, b_cols, arr, bcr, pair_list, pair_count, row_order)


def solution(mesh):
    placed = (
        P("row", "col", None, None, None),
        P("row", "col", None),
        P("row", "col", None, None, None),
        P("row", "col", None),
        P("row", "col", None, None, None),
        P("row", "col", None),
        P("row", None),
    )
    return jax.shard_map(
        functools.partial(per_device, mesh.shape["row"], mesh.shape["col"]),
        mesh=mesh,
        in_specs=placed,
        out_specs=P("row", "col"),
        check_vma=False,
    )
```

```python
import functools

import jax
import jax.numpy as jnp
from jax import lax
from jax.experimental import pallas as pl
from jax.experimental.pallas import tpu as pltpu
from jax.sharding import PartitionSpec as P

CROWS = 4
CCOLS = 8
STOPS = 4
CHUNKS = 8
UNROLL = 8
LAG = 3
DETOUR = 2
ACROSS_AT = 3
MESH = pl.DeviceIdType.MESH
ANY = pl.BlockSpec(memory_space=pl.ANY)
VMEM = pl.BlockSpec(memory_space=pltpu.VMEM)
SMEM = pl.BlockSpec(memory_space=pltpu.SMEM)


def tree(jt, half):
    if jt == 3:
        return (0, ((0, 1), (0, 2), (2, 3))) if half else (2, ((2, 3), (2, 0), (0, 1)))
    if jt == 2:
        return (0, ((0, 3), (0, 1), (1, 2))) if half else (1, ((1, 2), (1, 0), (0, 3)))
    if jt == 1:
        return (2, ((2, 3), (2, 0), (0, 1))) if half else (0, ((0, 1), (0, 2), (2, 3)))
    return (1, ((1, 2), (1, 3), (3, 0))) if half else (0, ((0, 3), (3, 1), (1, 2)))


def plan_of(y, j):
    jt = (j - y) % 4
    landing = tree(jt, j // 2)[0]
    relays = []
    for w in range(STOPS):
        jt = (j + w) % 4
        land, hops = tree(jt, (jt + y) % 4 // 2)
        depth = {land: 0}
        for src, dst in hops:
            depth[dst] = depth[src] + 1
        relays.append((depth[w], w, tuple(dst for src, dst in hops if src == w)))
    return landing, tuple(sorted(relays))


def gather_kernel(
    n_row, n_col, a, b, arow, bcol, ar, br, arr, bcr, am, tb,
    a_ss, a_rs, b_ss, b_rs, m_ss, m_rs, x_ss, x_rs, f_ss,
):
    r = lax.axis_index("row")
    c = lax.axis_index("col")
    j = lax.rem(r, 4)
    y = lax.rem(c, 4)
    mirror = lax.rem(c + 4, n_col)
    step = b.shape[0] // CHUNKS
    bar = pltpu.get_barrier_semaphore()

    def rc(src, dst, ss, rs, dev):
        return pltpu.make_async_remote_copy(
            src, dst, ss, rs, device_id=dev, device_id_type=MESH
        )

    def row(d):
        return lax.rem(r + d + n_row, n_row)

    def signal(dev):
        pl.semaphore_signal(bar, 1, device_id=dev, device_id_type=MESH)

    def a_dst(s):
        return lax.rem(c - r - s + 8 * n_col, n_col)

    for d in range(1, n_col):
        signal((r, lax.rem(c + d, n_col)))
    for s in range(STOPS):

        @pl.when(c + s != 0)
        def _():
            signal((lax.rem(r + c + s, n_row), c))
            signal((lax.rem(r - c - s + n_row, n_row), c))

    for d in (1, 2, 3):
        signal((row(d), c))
        signal((row(-d), c))
    far = c >= 4
    for w in range(STOPS):

        @pl.when(far)
        def _():
            signal((lax.rem(r + c + w, n_row), mirror))

    pl.semaphore_wait(
        bar,
        n_col - 1 + 2 * (STOPS - jnp.where(c == 0, 1, 0)) + 6 + jnp.where(far, 0, STOPS),
    )

    def chunk(k):
        return pl.ds(k * step, step)

    across = rc(a, am, x_ss.at[0], x_rs.at[0], (r, mirror))

    def detour_copy(i):
        part = pl.ds(i * step, step)
        return rc(b.at[chunk(CHUNKS - 1 - i)], tb.at[part], x_ss.at[1 + i], x_rs.at[1 + i], (r, mirror))

    @pl.when(far)
    def _():
        for i in range(DETOUR):
            detour_copy(i).start()

    across.start()

    def landing_copy(k, w, dev):
        return rc(b.at[chunk(k)], br.at[w, chunk(k)], b_ss.at[0, k], b_rs.at[w, k], dev)

    jt = lax.rem(j - y + 4, 4)
    half = j // 2
    landing = jnp.int32(0)
    for t in range(4):
        for h in range(2):
            landing = jnp.where((jt == t) & (half == h), tree(t, h)[0], landing)
    own_b = c == 0

    @pl.when(jnp.logical_not(own_b))
    def _():
        for k in range(CHUNKS - DETOUR):
            landing_copy(k, landing, (lax.rem(r - c - landing + n_row, n_row), c)).start()

    @pl.when((c > 0) & (c < 4))
    def _():
        for k in range(CHUNKS - DETOUR, CHUNKS):
            landing_copy(k, landing, (lax.rem(r - c - landing + n_row, n_row), c)).start()

    def far_copy(i):
        k = CHUNKS - 1 - i
        dev = (lax.rem(r - mirror - landing + n_row, n_row), mirror)
        return rc(
            tb.at[pl.ds(i * step, step)], br.at[landing, chunk(k)],
            f_ss.at[i], b_rs.at[landing, k], dev,
        )

    for s in range(STOPS):

        @pl.when(lax.rem(r + s, n_col) != 0)
        def _():
            rc(arow, arr.at[s], m_ss.at[s], m_rs.at[s], (r, a_dst(s))).start()

        @pl.when(c + s != 0)
        def _():
            rc(
                bcol, bcr.at[s], m_ss.at[STOPS + s], m_rs.at[STOPS + s],
                (lax.rem(r - c - s + n_row, n_row), c),
            ).start()

    def ring_copy(d, src):
        to = c - y + lax.rem(y + d, 4)
        stop = lax.rem(c - to - r + 8 * n_col, n_col)
        own = stop < 4
        stop = lax.rem(stop, 4)
        return own, rc(src, ar.at[stop], a_ss.at[d], a_rs.at[stop], (r, to))

    for d in (1, 3, 2):
        own, copy = ring_copy(d, a)

        @pl.when(own)
        def _():
            copy.start()

    @pl.when(jnp.logical_not(far))
    def _():
        for i in range(DETOUR):
            detour_copy(i).wait_recv()
            far_copy(i).start()

    def wait_recv(w, k):
        rc(br.at[w, chunk(k)], br.at[w, chunk(k)], b_ss.at[0, k], b_rs.at[w, k], (r, c)).wait_recv()

    def relay_copy(w, to, k, slot, own):
        src = b.at[chunk(k)] if own else br.at[w, chunk(k)]
        return rc(src, br.at[to, chunk(k)], b_ss.at[slot, k], b_rs.at[to, k], (row(w - to), c))

    def run(relays, own):
        slots = {}
        for _, w, dests in relays:
            for to in dests:
                slots[w, to] = len(slots) + 1
        events = sorted(
            (k + LAG * depth, depth, k, w, dests)
            for depth, w, dests in relays
            for k in range(CHUNKS)
        )
        for at, (_, depth, k, w, dests) in enumerate(events):
            mine = own and w == 0
            if not mine:
                wait_recv(w, k)
            for to in dests:
                relay_copy(w, to, k, slots[w, to], mine).start()
            if at == ACROSS_AT:
                across.wait_recv()
                for d in (1, 3, 2):
                    first, copy = ring_copy(d, am)

                    @pl.when(jnp.logical_not(first))
                    def _():
                        copy.start()

        for k in range(CHUNKS):
            slot = 1
            for _, w, dests in relays:
                for to in dests:
                    relay_copy(w, to, k, slot, own and w == 0).wait_send()
                    slot += 1

    for jj in range(4):
        for yy in range(4):
            for own in (False, True) if yy == 0 else (False,):
                here = (j == jj) & (y == yy)
                if yy == 0:
                    here = here & (own_b if own else jnp.logical_not(own_b))

                @pl.when(here)
                def _():
                    run(plan_of(yy, jj)[1], own)

    @pl.when(jnp.logical_not(own_b))
    def _():
        for k in range(CHUNKS - DETOUR):
            landing_copy(k, 0, (r, c)).wait_send()

    @pl.when((c > 0) & (c < 4))
    def _():
        for k in range(CHUNKS - DETOUR, CHUNKS):
            landing_copy(k, 0, (r, c)).wait_send()

    @pl.when(far)
    def _():
        for i in range(DETOUR):
            detour_copy(i).wait_send()

    @pl.when(jnp.logical_not(far))
    def _():
        for i in range(DETOUR):
            far_copy(i).wait_send()

    across.wait_send()
    for d in (1, 3, 2):
        ring_copy(d, a)[1].wait_send()
    for s in range(STOPS):

        @pl.when(lax.rem(r + s, 4) != 0)
        def _():
            rc(a, ar.at[s], a_ss.at[1], a_rs.at[s], (r, c)).wait_recv()

        @pl.when(lax.rem(r + s, n_col) != 0)
        def _():
            rc(arow, arr.at[s], m_ss.at[s], m_rs.at[s], (r, c)).wait()

        @pl.when(c + s != 0)
        def _():
            rc(bcol, bcr.at[s], m_ss.at[STOPS + s], m_rs.at[STOPS + s], (r, c)).wait()


def multiply_kernel(
    n_col, a, b, ar, br, am, arow, bcol, arr, bcr, pairs, count, order, out,
    avm, bvm, acc, codes_v, codes, a_sem, b_sem, c_sem,
):
    r = lax.axis_index("row")
    c = lax.axis_index("col")
    n_a = a.shape[0]
    n_b = b.shape[0]
    n_pairs = pairs.shape[-1]
    edge = acc.shape[1]
    n_t = CROWS * CCOLS

    for s in range(STOPS):
        a_to = avm.at[s, pl.ds(1, n_a)]

        @pl.when(lax.rem(r + s, n_col) == 0)
        def _():
            pltpu.make_async_copy(a, a_to, a_sem.at[s]).start()

        @pl.when(lax.rem(r + s, n_col) == 4)
        def _():
            pltpu.make_async_copy(am, a_to, a_sem.at[s]).start()

        @pl.when(lax.rem(r + s, 4) != 0)
        def _():
            pltpu.make_async_copy(ar.at[s], a_to, a_sem.at[s]).start()

        if s == 0:

            @pl.when(c == 0)
            def _():
                pltpu.make_async_copy(b, bvm.at[s], b_sem.at[s]).start()

            @pl.when(c != 0)
            def _():
                pltpu.make_async_copy(br.at[s], bvm.at[s], b_sem.at[s]).start()
        else:
            pltpu.make_async_copy(br.at[s], bvm.at[s], b_sem.at[s]).start()
        avm[s, 0] = jnp.zeros((edge, edge), avm.dtype)

    i32 = jnp.int32
    lane = lax.broadcasted_iota(i32, (1, n_pairs), 1)
    wide = codes_v.shape[1]
    stops = []
    for s in range(STOPS):
        rows = jnp.where(lax.rem(r + s, n_col) == 0, arow[0], arr[s, 0])
        cols = jnp.where(c + s == 0, bcol[0], bcr[s, 0])
        placed = jnp.zeros_like(rows)
        for i in range(CROWS):
            placed = placed + jnp.where(rows == i, order[0, i], 0)
        left = pairs[0, 0, s, 0:1, :]
        right = pairs[0, 0, s, 1:2, :]
        target = jnp.zeros_like(left)
        for l in range(n_a):
            target = target + jnp.where(left == l, placed[:, l : l + 1] * CCOLS, 0)
        for k in range(n_b):
            target = target + jnp.where(right == k, cols[:, k : k + 1], 0)
        live = lane < count[0, 0, s]
        stops.append(jnp.where(live, target, n_t))
        stops.append(target * 65536 + right * 256 + left + 1)
    table = jnp.concatenate(stops, axis=0).T
    here = lax.broadcasted_iota(i32, (n_pairs, n_pairs), 0)
    there = lax.broadcasted_iota(i32, (n_pairs, n_pairs), 1)
    earlier = there < here
    t_lane = lax.broadcasted_iota(i32, (n_pairs, 128), 1)
    slot = lax.broadcasted_iota(i32, (n_pairs, wide), 1)
    for s in range(STOPS):
        t_row = stops[2 * s]
        t_col = table[:, 2 * s : 2 * s + 1]
        code = table[:, 2 * s + 1 : 2 * s + 2]
        rank = jnp.sum(jnp.where((t_row == t_col) & earlier, 1, 0), axis=1, keepdims=True)
        held = jnp.sum(jnp.where(t_col == t_lane, 1, 0), axis=0, keepdims=True)
        held = jnp.where(t_lane[0:1] < n_t, (held + 1) // 2 * 2, 0)
        before = jnp.sum(jnp.where(t_lane < t_col, held, 0), axis=1, keepdims=True)
        place = jnp.where(t_col < n_t, before + rank, wide)
        codes_v[s : s + 1, :] = jnp.sum(jnp.where(place == slot, code, 0), axis=0, keepdims=True)
        total = jnp.sum(held, axis=1, keepdims=True)
        codes_v[STOPS + s : STOPS + s + 1, :] = jnp.broadcast_to(total, (1, wide))

    acc[...] = jnp.zeros_like(acc)
    listing = pltpu.make_async_copy(codes_v, codes, c_sem)
    listing.start()
    listing.wait()
    for s in range(STOPS):
        pltpu.make_async_copy(ar.at[s], avm.at[s, pl.ds(1, n_a)], a_sem.at[s]).wait()
        pltpu.make_async_copy(br.at[s], bvm.at[s], b_sem.at[s]).wait()
        steps = codes[STOPS + s, 0] // 2

        def body(t, carry):
            for u in range(UNROLL):
                at = (t * UNROLL + u) * 2
                one = codes[s, at]
                two = codes[s, at + 1]
                lhs = jnp.concatenate([avm[s, one & 255], avm[s, two & 255]], axis=1)
                rhs = jnp.concatenate(
                    [bvm[s, (one >> 8) & 255], bvm[s, (two >> 8) & 255]], axis=0
                )
                acc[one >> 16] += jnp.dot(lhs, rhs, preferred_element_type=jnp.float32)
            return carry

        lax.fori_loop(0, (steps + UNROLL - 1) // UNROLL, body, 0)
    for i in range(CROWS):
        for k in range(CCOLS):
            out[i * edge : (i + 1) * edge, k * edge : (k + 1) * edge] = acc[
                i * CCOLS + k
            ].astype(out.dtype)


def per_device(n_row, n_col, a_blocks, a_rows, b_blocks, b_cols, pair_list, pair_count, row_order):
    a = a_blocks[0, 0]
    b = b_blocks[0, 0]
    n_a, edge, _ = a.shape
    n_b = b.shape[0]
    dt = a.dtype
    dma = pltpu.SemaphoreType.DMA
    most = pair_list.shape[-1] + CROWS * CCOLS + 2 * UNROLL
    wide = (most + 127) // 128 * 128
    ar, br, arr, bcr, am, _ = pl.pallas_call(
        functools.partial(gather_kernel, n_row, n_col),
        out_shape=(
            jax.ShapeDtypeStruct((STOPS, n_a, edge, edge), dt),
            jax.ShapeDtypeStruct((STOPS, n_b, edge, edge), dt),
            jax.ShapeDtypeStruct((STOPS, 1, 1, n_a), jnp.int32),
            jax.ShapeDtypeStruct((STOPS, 1, 1, n_b), jnp.int32),
            jax.ShapeDtypeStruct((n_a, edge, edge), dt),
            jax.ShapeDtypeStruct((DETOUR * n_b // CHUNKS, edge, edge), dt),
        ),
        in_specs=[ANY] * 4,
        out_specs=(ANY,) * 6,
        scratch_shapes=[
            dma((STOPS,)),
            dma((STOPS,)),
            dma((8, CHUNKS)),
            dma((STOPS, CHUNKS)),
            dma((2 * STOPS,)),
            dma((2 * STOPS,)),
            dma((1 + DETOUR,)),
            dma((1 + DETOUR,)),
            dma((DETOUR,)),
        ],
        compiler_params=pltpu.CompilerParams(collective_id=0, has_side_effects=True),
        name="gather",
    )(a, b, a_rows, b_cols)
    return pl.pallas_call(
        functools.partial(multiply_kernel, n_col),
        out_shape=jax.ShapeDtypeStruct((CROWS * edge, CCOLS * edge), dt),
        in_specs=[ANY] * 5 + [VMEM] * 5 + [SMEM] * 2,
        out_specs=pl.BlockSpec(memory_space=pltpu.VMEM),
        scratch_shapes=[
            pltpu.VMEM((STOPS, n_a + 1, edge, edge), dt),
            pltpu.VMEM((STOPS, n_b, edge, edge), dt),
            pltpu.VMEM((CROWS * CCOLS, edge, edge), jnp.float32),
            pltpu.VMEM((2 * STOPS, wide), jnp.int32),
            pltpu.SMEM((2 * STOPS, wide), jnp.int32),
            dma((STOPS,)),
            dma((STOPS,)),
            dma,
        ],
        name="multiply",
    )(a, b, ar, br, am, a_rows, b_cols, arr, bcr, pair_list, pair_count, row_order)


def solution(mesh):
    placed = (
        P("row", "col", None, None, None),
        P("row", "col", None),
        P("row", "col", None, None, None),
        P("row", "col", None),
        P("row", "col", None, None, None),
        P("row", "col", None),
        P("row", None),
    )
    return jax.shard_map(
        functools.partial(per_device, mesh.shape["row"], mesh.shape["col"]),
        mesh=mesh,
        in_specs=placed,
        out_specs=P("row", "col"),
        check_vma=False,
    )
```

```python
import functools

import jax
import jax.numpy as jnp
from jax import lax
from jax.experimental import pallas as pl
from jax.experimental.pallas import tpu as pltpu
from jax.sharding import PartitionSpec as P

CROWS = 4
CCOLS = 8
STOPS = 4
CHUNKS = 8
UNROLL = 32
LAG = 4
DETOUR = 2
DETOUR_K = 4
FIRST = 3
A_CHUNKS = 4
ACROSS_AT = 1
ACROSS_BY = 2
MESH = pl.DeviceIdType.MESH
ANY = pl.BlockSpec(memory_space=pl.ANY)
VMEM = pl.BlockSpec(memory_space=pltpu.VMEM)
SMEM = pl.BlockSpec(memory_space=pltpu.SMEM)


def tree(jt, half):
    if jt == 3:
        return (0, ((0, 1), (0, 2), (2, 3))) if half else (2, ((2, 3), (2, 0), (0, 1)))
    if jt == 2:
        return (0, ((0, 3), (0, 1), (1, 2))) if half else (1, ((1, 2), (1, 0), (0, 3)))
    if jt == 1:
        return (2, ((2, 3), (2, 0), (0, 1))) if half else (0, ((0, 1), (0, 2), (2, 3)))
    return (1, ((1, 2), (1, 3), (3, 0))) if half else (0, ((0, 3), (3, 1), (1, 2)))


def plan_of(y, j):
    jt = (j - y) % 4
    landing = tree(jt, j // 2)[0]
    relays = []
    for w in range(STOPS):
        jt = (j + w) % 4
        land, hops = tree(jt, (jt + y) % 4 // 2)
        depth = {land: 0}
        for src, dst in hops:
            depth[dst] = depth[src] + 1
        relays.append((depth[w], w, tuple(dst for src, dst in hops if src == w)))
    return landing, tuple(sorted(relays))


def gather_kernel(
    n_row, n_col, a, b, arow, bcol, ar, br, arr, bcr, am, tb,
    a_ss, a_rs, b_ss, b_rs, m_ss, m_rs, x_ss, x_rs, f_ss,
):
    r = lax.axis_index("row")
    c = lax.axis_index("col")
    j = lax.rem(r, 4)
    y = lax.rem(c, 4)
    mirror = lax.rem(c + 4, n_col)
    partner = n_col - 1 - c
    step = b.shape[0] // CHUNKS
    bar = pltpu.get_barrier_semaphore()

    def rc(src, dst, ss, rs, dev):
        return pltpu.make_async_remote_copy(
            src, dst, ss, rs, device_id=dev, device_id_type=MESH
        )

    def row(d):
        return lax.rem(r + d + n_row, n_row)

    def signal(dev):
        pl.semaphore_signal(bar, 1, device_id=dev, device_id_type=MESH)

    def a_dst(s):
        return lax.rem(c - r - s + 8 * n_col, n_col)

    for d in range(1, n_col):
        signal((r, lax.rem(c + d, n_col)))
    for s in range(STOPS):

        @pl.when(c + s != 0)
        def _():
            signal((lax.rem(r + c + s, n_row), c))
            signal((lax.rem(r - c - s + n_row, n_row), c))

    for d in (1, 2, 3):
        signal((row(d), c))
        signal((row(-d), c))
    far = c >= 4
    detours = (lax.max(c, partner) - 2) // 2
    for w in range(STOPS):

        @pl.when(far)
        def _():
            signal((lax.rem(r + c + w, n_row), partner))

    pl.semaphore_wait(
        bar,
        n_col - 1 + 2 * (STOPS - jnp.where(c == 0, 1, 0)) + 6 + jnp.where(far, 0, STOPS),
    )

    def chunk(k):
        return pl.ds(k * step, step)

    a_step = a.shape[0] // A_CHUNKS

    def a_chunk(q):
        return pl.ds(q * a_step, a_step)

    def across(q):
        return rc(a.at[a_chunk(q)], am.at[a_chunk(q)], x_ss.at[q], x_rs.at[q], (r, mirror))


    def detour_copy(i):
        part = pl.ds(i * step, step)
        return rc(b.at[chunk(DETOUR_K + i)], tb.at[part], x_ss.at[A_CHUNKS + i], x_rs.at[A_CHUNKS + i], (r, partner))

    for i in range(DETOUR):

        @pl.when(far & (i < detours))
        def _():
            detour_copy(i).start()

    for q in range(A_CHUNKS):
        across(q).start()

    def landing_copy(k, w, dev):
        return rc(b.at[chunk(k)], br.at[w, chunk(k)], b_ss.at[0, k], b_rs.at[w, k], dev)

    def landing_of(column):
        jt = lax.rem(j - column + 4, 4)
        found = jnp.int32(0)
        for t in range(4):
            for h in range(2):
                found = jnp.where((jt == t) & (j // 2 == h), tree(t, h)[0], found)
        return found

    landing = landing_of(y)
    partner_landing = landing_of(3 - y)
    own_b = c == 0

    def direct(k):
        return jnp.logical_not(own_b) & (
            jnp.logical_not(far) | (k < DETOUR_K) | (k - DETOUR_K >= detours)
        )

    def send_right(k):
        @pl.when(direct(k))
        def _():
            landing_copy(k, landing, (lax.rem(r - c - landing + n_row, n_row), c)).start()

    for k in range(FIRST):
        send_right(k)

    def far_copy(i):
        k = DETOUR_K + i
        dev = (lax.rem(r - partner - partner_landing + n_row, n_row), partner)
        return rc(
            tb.at[pl.ds(i * step, step)], br.at[partner_landing, chunk(k)],
            f_ss.at[i], b_rs.at[partner_landing, k], dev,
        )

    for s in range(STOPS):

        @pl.when(lax.rem(r + s, n_col) != 0)
        def _():
            rc(arow, arr.at[s], m_ss.at[s], m_rs.at[s], (r, a_dst(s))).start()

        @pl.when(c + s != 0)
        def _():
            rc(
                bcol, bcr.at[s], m_ss.at[STOPS + s], m_rs.at[STOPS + s],
                (lax.rem(r - c - s + n_row, n_row), c),
            ).start()

    def ring_copy(d, src, q):
        to = c - y + lax.rem(y + d, 4)
        stop = lax.rem(c - to - r + 8 * n_col, n_col)
        own = stop < 4
        stop = lax.rem(stop, 4)
        return own, rc(
            src.at[a_chunk(q)], ar.at[stop, a_chunk(q)], a_ss.at[d, q], a_rs.at[stop, q], (r, to)
        )

    for d in (1, 3, 2):
        for q in range(A_CHUNKS):
            own, copy = ring_copy(d, a, q)

            @pl.when(own)
            def _():
                copy.start()

    for i in range(DETOUR):

        @pl.when(jnp.logical_not(far) & (i < detours))
        def _():
            detour_copy(i).wait_recv()
            far_copy(i).start()

        if i == 0:
            for k in range(FIRST, CHUNKS):
                send_right(k)

    def wait_recv(w, k):
        rc(br.at[w, chunk(k)], br.at[w, chunk(k)], b_ss.at[0, k], b_rs.at[w, k], (r, c)).wait_recv()

    def relay_copy(w, to, k, slot, own):
        src = b.at[chunk(k)] if own else br.at[w, chunk(k)]
        return rc(src, br.at[to, chunk(k)], b_ss.at[slot, k], b_rs.at[to, k], (row(w - to), c))

    def run(relays, own):
        slots = {}
        for _, w, dests in relays:
            for to in dests:
                slots[w, to] = len(slots) + 1
        events = sorted(
            (k + LAG * depth, depth, k, w, dests)
            for depth, w, dests in relays
            for k in range(CHUNKS)
        )
        def relay_left(q):
            across(q).wait_recv()
            for d in (1, 3, 2):
                first, copy = ring_copy(d, am, q)

                @pl.when(jnp.logical_not(first))
                def _():
                    copy.start()

        extra = []
        for q in range(A_CHUNKS):
            extra.append((ACROSS_AT + q * ACROSS_BY, functools.partial(relay_left, q)))
        for at in range(max(len(events), 1 + max(e[0] for e in extra))):
            if at < len(events):
                _, depth, k, w, dests = events[at]
                mine = own and w == 0
                if not mine:
                    wait_recv(w, k)
                for to in dests:
                    relay_copy(w, to, k, slots[w, to], mine).start()
            for when, action in extra:
                if when == at:
                    action()

        for k in range(CHUNKS):
            slot = 1
            for _, w, dests in relays:
                for to in dests:
                    relay_copy(w, to, k, slot, own and w == 0).wait_send()
                    slot += 1

    for jj in range(4):
        for yy in range(4):
            for own in (False, True) if yy == 0 else (False,):
                here = (j == jj) & (y == yy)
                if yy == 0:
                    here = here & (own_b if own else jnp.logical_not(own_b))

                @pl.when(here)
                def _():
                    run(plan_of(yy, jj)[1], own)

    for k in range(CHUNKS):

        @pl.when(direct(k))
        def _():
            landing_copy(k, 0, (r, c)).wait_send()

    for i in range(DETOUR):

        @pl.when(far & (i < detours))
        def _():
            detour_copy(i).wait_send()

        @pl.when(jnp.logical_not(far) & (i < detours))
        def _():
            far_copy(i).wait_send()

    for q in range(A_CHUNKS):
        across(q).wait_send()
        for d in (1, 3, 2):
            ring_copy(d, a, q)[1].wait_send()
    for s in range(STOPS):

        @pl.when(lax.rem(r + s, 4) != 0)
        def _():
            for q in range(A_CHUNKS):
                part = ar.at[s, a_chunk(q)]
                rc(part, part, a_ss.at[1, q], a_rs.at[s, q], (r, c)).wait_recv()

        @pl.when(lax.rem(r + s, n_col) != 0)
        def _():
            rc(arow, arr.at[s], m_ss.at[s], m_rs.at[s], (r, c)).wait()

        @pl.when(c + s != 0)
        def _():
            rc(bcol, bcr.at[s], m_ss.at[STOPS + s], m_rs.at[STOPS + s], (r, c)).wait()


def multiply_kernel(
    n_col, a, b, ar, br, am, arow, bcol, arr, bcr, pairs, count, order, out,
    avm, bvm, acc, codes_v, codes, a_sem, b_sem, c_sem,
):
    r = lax.axis_index("row")
    c = lax.axis_index("col")
    n_a = a.shape[0]
    n_b = b.shape[0]
    n_pairs = pairs.shape[-1]
    edge = acc.shape[1]
    n_t = CROWS * CCOLS

    for s in range(STOPS):
        a_to = avm.at[pl.ds(1 + s * n_a, n_a)]

        @pl.when(lax.rem(r + s, n_col) == 0)
        def _():
            pltpu.make_async_copy(a, a_to, a_sem.at[s]).start()

        @pl.when(lax.rem(r + s, n_col) == 4)
        def _():
            pltpu.make_async_copy(am, a_to, a_sem.at[s]).start()

        @pl.when(lax.rem(r + s, 4) != 0)
        def _():
            pltpu.make_async_copy(ar.at[s], a_to, a_sem.at[s]).start()

        if s == 0:

            @pl.when(c == 0)
            def _():
                pltpu.make_async_copy(b, bvm.at[pl.ds(s * n_b, n_b)], b_sem.at[s]).start()

            @pl.when(c != 0)
            def _():
                pltpu.make_async_copy(br.at[s], bvm.at[pl.ds(s * n_b, n_b)], b_sem.at[s]).start()
        else:
            pltpu.make_async_copy(br.at[s], bvm.at[pl.ds(s * n_b, n_b)], b_sem.at[s]).start()
    avm[0] = jnp.zeros((edge, edge), avm.dtype)

    i32 = jnp.int32
    lane = lax.broadcasted_iota(i32, (1, n_pairs), 1)
    wide = codes_v.shape[1]
    stops = []
    for s in range(STOPS):
        rows = jnp.where(lax.rem(r + s, n_col) == 0, arow[0], arr[s, 0])
        cols = jnp.where(c + s == 0, bcol[0], bcr[s, 0])
        placed = jnp.zeros_like(rows)
        for i in range(CROWS):
            placed = placed + jnp.where(rows == i, order[0, i], 0)
        left = pairs[0, 0, s, 0:1, :]
        right = pairs[0, 0, s, 1:2, :]
        target = jnp.zeros_like(left)
        for l in range(n_a):
            target = target + jnp.where(left == l, placed[:, l : l + 1] * CCOLS, 0)
        for k in range(n_b):
            target = target + jnp.where(right == k, cols[:, k : k + 1], 0)
        live = lane < count[0, 0, s]
        stops.append(jnp.where(live, target, n_t))
        stops.append(target * 65536 + (right + s * n_b) * 256 + left + s * n_a + 1)
    table = jnp.concatenate(stops, axis=0).T
    here = lax.broadcasted_iota(i32, (n_pairs, n_pairs), 0)
    there = lax.broadcasted_iota(i32, (n_pairs, n_pairs), 1)
    earlier = there < here
    t_lane = lax.broadcasted_iota(i32, (n_pairs, 128), 1)
    slot = lax.broadcasted_iota(i32, (n_pairs, wide), 1)
    base = jnp.zeros((1, 1), i32)
    listed = jnp.zeros((1, wide), i32)
    for s in range(STOPS):
        t_row = stops[2 * s]
        t_col = table[:, 2 * s : 2 * s + 1]
        code = table[:, 2 * s + 1 : 2 * s + 2]
        rank = jnp.sum(jnp.where((t_row == t_col) & earlier, 1, 0), axis=1, keepdims=True)
        held = jnp.sum(jnp.where(t_col == t_lane, 1, 0), axis=0, keepdims=True)
        held = jnp.where(t_lane[0:1] < n_t, (held + 1) // 2 * 2, 0)
        before = jnp.sum(jnp.where(t_lane < t_col, held, 0), axis=1, keepdims=True)
        place = jnp.where(t_col < n_t, base + before + rank, wide)
        listed = listed + jnp.sum(jnp.where(place == slot, code, 0), axis=0, keepdims=True)
        base = base + jnp.sum(held, axis=1, keepdims=True)
    codes_v[0:1, :] = listed
    codes_v[1:2, :] = jnp.broadcast_to(base, (1, wide))

    acc[...] = jnp.zeros_like(acc)
    listing = pltpu.make_async_copy(codes_v, codes, c_sem)
    listing.start()
    listing.wait()
    for s in range(STOPS):
        pltpu.make_async_copy(ar.at[s], avm.at[pl.ds(1 + s * n_a, n_a)], a_sem.at[s]).wait()
        pltpu.make_async_copy(br.at[s], bvm.at[pl.ds(s * n_b, n_b)], b_sem.at[s]).wait()

    def body(t, carry):
        for u in range(UNROLL):
            at = (t * UNROLL + u) * 2
            one = codes[0, at]
            two = codes[0, at + 1]
            lhs = jnp.concatenate([avm[one & 255], avm[two & 255]], axis=1)
            rhs = jnp.concatenate([bvm[(one >> 8) & 255], bvm[(two >> 8) & 255]], axis=0)
            acc[one >> 16] += jnp.dot(lhs, rhs, preferred_element_type=jnp.float32)
        return carry

    steps = codes[1, 0] // 2
    lax.fori_loop(0, (steps + UNROLL - 1) // UNROLL, body, 0)
    for i in range(CROWS):
        for k in range(CCOLS):
            out[i * edge : (i + 1) * edge, k * edge : (k + 1) * edge] = acc[
                i * CCOLS + k
            ].astype(out.dtype)


def per_device(n_row, n_col, a_blocks, a_rows, b_blocks, b_cols, pair_list, pair_count, row_order):
    a = a_blocks[0, 0]
    b = b_blocks[0, 0]
    n_a, edge, _ = a.shape
    n_b = b.shape[0]
    dt = a.dtype
    dma = pltpu.SemaphoreType.DMA
    most = STOPS * (pair_list.shape[-1] + CROWS * CCOLS) + 2 * UNROLL
    wide = (most + 127) // 128 * 128
    ar, br, arr, bcr, am, _ = pl.pallas_call(
        functools.partial(gather_kernel, n_row, n_col),
        out_shape=(
            jax.ShapeDtypeStruct((STOPS, n_a, edge, edge), dt),
            jax.ShapeDtypeStruct((STOPS, n_b, edge, edge), dt),
            jax.ShapeDtypeStruct((STOPS, 1, 1, n_a), jnp.int32),
            jax.ShapeDtypeStruct((STOPS, 1, 1, n_b), jnp.int32),
            jax.ShapeDtypeStruct((n_a, edge, edge), dt),
            jax.ShapeDtypeStruct((DETOUR * n_b // CHUNKS, edge, edge), dt),
        ),
        in_specs=[ANY] * 4,
        out_specs=(ANY,) * 6,
        scratch_shapes=[
            dma((4, A_CHUNKS)),
            dma((STOPS, A_CHUNKS)),
            dma((8, CHUNKS)),
            dma((STOPS, CHUNKS)),
            dma((2 * STOPS,)),
            dma((2 * STOPS,)),
            dma((A_CHUNKS + DETOUR,)),
            dma((A_CHUNKS + DETOUR,)),
            dma((DETOUR,)),
        ],
        compiler_params=pltpu.CompilerParams(collective_id=0, has_side_effects=True),
        name="gather",
    )(a, b, a_rows, b_cols)
    return pl.pallas_call(
        functools.partial(multiply_kernel, n_col),
        out_shape=jax.ShapeDtypeStruct((CROWS * edge, CCOLS * edge), dt),
        in_specs=[ANY] * 5 + [VMEM] * 5 + [SMEM] * 2,
        out_specs=pl.BlockSpec(memory_space=pltpu.VMEM),
        scratch_shapes=[
            pltpu.VMEM((STOPS * n_a + 1, edge, edge), dt),
            pltpu.VMEM((STOPS * n_b, edge, edge), dt),
            pltpu.VMEM((CROWS * CCOLS, edge, edge), jnp.float32),
            pltpu.VMEM((8, wide), jnp.int32),
            pltpu.SMEM((8, wide), jnp.int32),
            dma((STOPS,)),
            dma((STOPS,)),
            dma,
        ],
        name="multiply",
    )(a, b, ar, br, am, a_rows, b_cols, arr, bcr, pair_list, pair_count, row_order)


def solution(mesh):
    placed = (
        P("row", "col", None, None, None),
        P("row", "col", None),
        P("row", "col", None, None, None),
        P("row", "col", None),
        P("row", "col", None, None, None),
        P("row", "col", None),
        P("row", None),
    )
    return jax.shard_map(
        functools.partial(per_device, mesh.shape["row"], mesh.shape["col"]),
        mesh=mesh,
        in_specs=placed,
        out_specs=P("row", "col"),
        check_vma=False,
    )
```

```python
import functools

import jax
import jax.numpy as jnp
from jax import lax
from jax.experimental import pallas as pl
from jax.experimental.pallas import tpu as pltpu
from jax.sharding import PartitionSpec as P

CROWS = 4
CCOLS = 8
STOPS = 4
CHUNKS = 8
UNROLL = 32
GROUP = 2
LAG = 4
DETOUR = 2
DETOUR_K = 3
FIRST = 3
A_CHUNKS = 4
ACROSS_AT = 1
ACROSS_BY = 2
MESH = pl.DeviceIdType.MESH
ANY = pl.BlockSpec(memory_space=pl.ANY)
VMEM = pl.BlockSpec(memory_space=pltpu.VMEM)
SMEM = pl.BlockSpec(memory_space=pltpu.SMEM)


def tree(jt, half):
    if jt == 3:
        return (0, ((0, 1), (0, 2), (2, 3))) if half else (2, ((2, 3), (2, 0), (0, 1)))
    if jt == 2:
        return (0, ((0, 3), (0, 1), (1, 2))) if half else (1, ((1, 2), (1, 0), (0, 3)))
    if jt == 1:
        return (2, ((2, 3), (2, 0), (0, 1))) if half else (0, ((0, 1), (0, 2), (2, 3)))
    return (1, ((1, 2), (1, 3), (3, 0))) if half else (0, ((0, 3), (3, 1), (1, 2)))


def plan_of(y, j):
    jt = (j - y) % 4
    landing = tree(jt, j // 2)[0]
    relays = []
    for w in range(STOPS):
        jt = (j + w) % 4
        land, hops = tree(jt, (jt + y) % 4 // 2)
        depth = {land: 0}
        for src, dst in hops:
            depth[dst] = depth[src] + 1
        relays.append((depth[w], w, tuple(dst for src, dst in hops if src == w)))
    return landing, tuple(sorted(relays))


def gather_kernel(
    n_row, n_col, a, b, arow, bcol, ar, br, arr, bcr, am, tb,
    a_ss, a_rs, b_ss, b_rs, m_ss, m_rs, x_ss, x_rs, f_ss,
):
    r = lax.axis_index("row")
    c = lax.axis_index("col")
    j = lax.rem(r, 4)
    y = lax.rem(c, 4)
    mirror = lax.rem(c + 4, n_col)
    partner = n_col - 1 - c
    step = b.shape[0] // CHUNKS
    bar = pltpu.get_barrier_semaphore()

    def rc(src, dst, ss, rs, dev):
        return pltpu.make_async_remote_copy(
            src, dst, ss, rs, device_id=dev, device_id_type=MESH
        )

    def row(d):
        return lax.rem(r + d + n_row, n_row)

    def signal(dev):
        pl.semaphore_signal(bar, 1, device_id=dev, device_id_type=MESH)

    def a_dst(s):
        return lax.rem(c - r - s + 8 * n_col, n_col)

    for d in range(1, n_col):
        signal((r, lax.rem(c + d, n_col)))
    for s in range(STOPS):

        @pl.when(c + s != 0)
        def _():
            signal((lax.rem(r + c + s, n_row), c))
            signal((lax.rem(r - c - s + n_row, n_row), c))

    for d in (1, 2, 3):
        signal((row(d), c))
        signal((row(-d), c))
    far = c >= 4
    detours = (lax.max(c, partner) - 2) // 2
    for w in range(STOPS):

        @pl.when(far)
        def _():
            signal((lax.rem(r + c + w, n_row), partner))

    pl.semaphore_wait(
        bar,
        n_col - 1 + 2 * (STOPS - jnp.where(c == 0, 1, 0)) + 6 + jnp.where(far, 0, STOPS),
    )

    def chunk(k):
        return pl.ds(k * step, step)

    a_step = a.shape[0] // A_CHUNKS

    def a_chunk(q):
        return pl.ds(q * a_step, a_step)

    def across(q):
        return rc(a.at[a_chunk(q)], am.at[a_chunk(q)], x_ss.at[q], x_rs.at[q], (r, mirror))


    def detour_copy(i):
        part = pl.ds(i * step, step)
        return rc(b.at[chunk(DETOUR_K + i)], tb.at[part], x_ss.at[A_CHUNKS + i], x_rs.at[A_CHUNKS + i], (r, partner))

    for i in range(DETOUR):

        @pl.when(far & (i < detours))
        def _():
            detour_copy(i).start()

    for q in range(A_CHUNKS):
        across(q).start()

    def landing_copy(k, w, dev):
        return rc(b.at[chunk(k)], br.at[w, chunk(k)], b_ss.at[0, k], b_rs.at[w, k], dev)

    def landing_of(column):
        jt = lax.rem(j - column + 4, 4)
        found = jnp.int32(0)
        for t in range(4):
            for h in range(2):
                found = jnp.where((jt == t) & (j // 2 == h), tree(t, h)[0], found)
        return found

    landing = landing_of(y)
    partner_landing = landing_of(3 - y)
    own_b = c == 0

    def direct(k):
        return jnp.logical_not(own_b) & (
            jnp.logical_not(far) | (k < DETOUR_K) | (k - DETOUR_K >= detours)
        )

    def send_right(k):
        @pl.when(direct(k))
        def _():
            landing_copy(k, landing, (lax.rem(r - c - landing + n_row, n_row), c)).start()

    for k in range(FIRST):
        send_right(k)

    def far_copy(i):
        k = DETOUR_K + i
        dev = (lax.rem(r - partner - partner_landing + n_row, n_row), partner)
        return rc(
            tb.at[pl.ds(i * step, step)], br.at[partner_landing, chunk(k)],
            f_ss.at[i], b_rs.at[partner_landing, k], dev,
        )

    for s in range(STOPS):

        @pl.when(lax.rem(r + s, n_col) != 0)
        def _():
            rc(arow, arr.at[s], m_ss.at[s], m_rs.at[s], (r, a_dst(s))).start()

        @pl.when(c + s != 0)
        def _():
            rc(
                bcol, bcr.at[s], m_ss.at[STOPS + s], m_rs.at[STOPS + s],
                (lax.rem(r - c - s + n_row, n_row), c),
            ).start()

    def ring_copy(d, src, q):
        to = c - y + lax.rem(y + d, 4)
        stop = lax.rem(c - to - r + 8 * n_col, n_col)
        own = stop < 4
        stop = lax.rem(stop, 4)
        return own, rc(
            src.at[a_chunk(q)], ar.at[stop, a_chunk(q)], a_ss.at[d, q], a_rs.at[stop, q], (r, to)
        )

    for d in (1, 3, 2):
        for q in range(A_CHUNKS):
            own, copy = ring_copy(d, a, q)

            @pl.when(own)
            def _():
                copy.start()

    for i in range(DETOUR):

        @pl.when(jnp.logical_not(far) & (i < detours))
        def _():
            detour_copy(i).wait_recv()
            far_copy(i).start()

        if i == 0:
            for k in range(FIRST, CHUNKS):
                send_right(k)

    def wait_recv(w, k):
        rc(br.at[w, chunk(k)], br.at[w, chunk(k)], b_ss.at[0, k], b_rs.at[w, k], (r, c)).wait_recv()

    def relay_copy(w, to, k, slot, own):
        src = b.at[chunk(k)] if own else br.at[w, chunk(k)]
        return rc(src, br.at[to, chunk(k)], b_ss.at[slot, k], b_rs.at[to, k], (row(w - to), c))

    def run(relays, own):
        slots = {}
        for _, w, dests in relays:
            for to in dests:
                slots[w, to] = len(slots) + 1
        events = sorted(
            (k + LAG * depth, depth, k, w, dests)
            for depth, w, dests in relays
            for k in range(CHUNKS)
        )
        def relay_left(q):
            across(q).wait_recv()
            for d in (1, 3, 2):
                first, copy = ring_copy(d, am, q)

                @pl.when(jnp.logical_not(first))
                def _():
                    copy.start()

        extra = []
        for q in range(A_CHUNKS):
            extra.append((ACROSS_AT + q * ACROSS_BY, functools.partial(relay_left, q)))
        for at in range(max(len(events), 1 + max(e[0] for e in extra))):
            if at < len(events):
                _, depth, k, w, dests = events[at]
                mine = own and w == 0
                if not mine:
                    wait_recv(w, k)
                for to in dests:
                    relay_copy(w, to, k, slots[w, to], mine).start()
            for when, action in extra:
                if when == at:
                    action()

        for k in range(CHUNKS):
            slot = 1
            for _, w, dests in relays:
                for to in dests:
                    relay_copy(w, to, k, slot, own and w == 0).wait_send()
                    slot += 1

    for jj in range(4):
        for yy in range(4):
            for own in (False, True) if yy == 0 else (False,):
                here = (j == jj) & (y == yy)
                if yy == 0:
                    here = here & (own_b if own else jnp.logical_not(own_b))

                @pl.when(here)
                def _():
                    run(plan_of(yy, jj)[1], own)

    for k in range(CHUNKS):

        @pl.when(direct(k))
        def _():
            landing_copy(k, 0, (r, c)).wait_send()

    for i in range(DETOUR):

        @pl.when(far & (i < detours))
        def _():
            detour_copy(i).wait_send()

        @pl.when(jnp.logical_not(far) & (i < detours))
        def _():
            far_copy(i).wait_send()

    for q in range(A_CHUNKS):
        across(q).wait_send()
        for d in (1, 3, 2):
            ring_copy(d, a, q)[1].wait_send()
    for s in range(STOPS):

        @pl.when(lax.rem(r + s, 4) != 0)
        def _():
            for q in range(A_CHUNKS):
                part = ar.at[s, a_chunk(q)]
                rc(part, part, a_ss.at[1, q], a_rs.at[s, q], (r, c)).wait_recv()

        @pl.when(lax.rem(r + s, n_col) != 0)
        def _():
            rc(arow, arr.at[s], m_ss.at[s], m_rs.at[s], (r, c)).wait()

        @pl.when(c + s != 0)
        def _():
            rc(bcol, bcr.at[s], m_ss.at[STOPS + s], m_rs.at[STOPS + s], (r, c)).wait()


def multiply_kernel(
    n_col, a, b, ar, br, am, arow, bcol, arr, bcr, pairs, count, order, out,
    avm, bvm, acc, codes_v, codes, a_sem, b_sem, c_sem,
):
    r = lax.axis_index("row")
    c = lax.axis_index("col")
    n_a = a.shape[0]
    n_b = b.shape[0]
    n_pairs = pairs.shape[-1]
    edge = acc.shape[1]
    n_t = CROWS * CCOLS

    for s in range(STOPS):
        a_to = avm.at[pl.ds(1 + s * n_a, n_a)]

        @pl.when(lax.rem(r + s, n_col) == 0)
        def _():
            pltpu.make_async_copy(a, a_to, a_sem.at[s]).start()

        @pl.when(lax.rem(r + s, n_col) == 4)
        def _():
            pltpu.make_async_copy(am, a_to, a_sem.at[s]).start()

        @pl.when(lax.rem(r + s, 4) != 0)
        def _():
            pltpu.make_async_copy(ar.at[s], a_to, a_sem.at[s]).start()

        if s == 0:

            @pl.when(c == 0)
            def _():
                pltpu.make_async_copy(b, bvm.at[pl.ds(s * n_b, n_b)], b_sem.at[s]).start()

            @pl.when(c != 0)
            def _():
                pltpu.make_async_copy(br.at[s], bvm.at[pl.ds(s * n_b, n_b)], b_sem.at[s]).start()
        else:
            pltpu.make_async_copy(br.at[s], bvm.at[pl.ds(s * n_b, n_b)], b_sem.at[s]).start()
    avm[0] = jnp.zeros((edge, edge), avm.dtype)

    i32 = jnp.int32
    lane = lax.broadcasted_iota(i32, (1, n_pairs), 1)
    wide = codes_v.shape[1]
    stops = []
    for s in range(STOPS):
        rows = jnp.where(lax.rem(r + s, n_col) == 0, arow[0], arr[s, 0])
        cols = jnp.where(c + s == 0, bcol[0], bcr[s, 0])
        placed = jnp.zeros_like(rows)
        for i in range(CROWS):
            placed = placed + jnp.where(rows == i, order[0, i], 0)
        left = pairs[0, 0, s, 0:1, :]
        right = pairs[0, 0, s, 1:2, :]
        target = jnp.zeros_like(left)
        for l in range(n_a):
            target = target + jnp.where(left == l, placed[:, l : l + 1] * CCOLS, 0)
        for k in range(n_b):
            target = target + jnp.where(right == k, cols[:, k : k + 1], 0)
        live = lane < count[0, 0, s]
        stops.append(jnp.where(live, target, n_t))
        stops.append(target * 65536 + (right + s * n_b) * 256 + left + s * n_a + 1)
    table = jnp.concatenate(stops, axis=0).T
    here = lax.broadcasted_iota(i32, (n_pairs, n_pairs), 0)
    there = lax.broadcasted_iota(i32, (n_pairs, n_pairs), 1)
    earlier = there < here
    t_lane = lax.broadcasted_iota(i32, (n_pairs, 128), 1)
    slot = lax.broadcasted_iota(i32, (n_pairs, wide), 1)
    listed = jnp.zeros((1, wide), i32)
    total = jnp.zeros((1, 128), i32)
    earlier_stops = []
    for s in range(STOPS):
        earlier_stops.append(total)
        t_col = table[:, 2 * s : 2 * s + 1]
        total = total + jnp.sum(jnp.where(t_col == t_lane, 1, 0), axis=0, keepdims=True)
    held = jnp.where(t_lane[0:1] < n_t, (total + GROUP - 1) // GROUP * GROUP, 0)
    for s in range(STOPS):
        t_row = stops[2 * s]
        t_col = table[:, 2 * s : 2 * s + 1]
        code = table[:, 2 * s + 1 : 2 * s + 2]
        rank = jnp.sum(jnp.where((t_row == t_col) & earlier, 1, 0), axis=1, keepdims=True)
        ahead = jnp.where(t_lane < t_col, held, jnp.where(t_lane == t_col, earlier_stops[s], 0))
        before = jnp.sum(ahead, axis=1, keepdims=True)
        place = jnp.where(t_col < n_t, before + rank, wide)
        listed = listed + jnp.sum(jnp.where(place == slot, code, 0), axis=0, keepdims=True)
    codes_v[0:1, :] = listed
    codes_v[1:2, :] = jnp.broadcast_to(jnp.sum(held, axis=1, keepdims=True), (1, wide))

    acc[...] = jnp.zeros_like(acc)
    listing = pltpu.make_async_copy(codes_v, codes, c_sem)
    listing.start()
    listing.wait()
    for s in range(STOPS):
        pltpu.make_async_copy(ar.at[s], avm.at[pl.ds(1 + s * n_a, n_a)], a_sem.at[s]).wait()
        pltpu.make_async_copy(br.at[s], bvm.at[pl.ds(s * n_b, n_b)], b_sem.at[s]).wait()

    def body(t, carry):
        for u in range(UNROLL):
            at = (t * UNROLL + u) * GROUP
            picks = [codes[0, at + g] for g in range(GROUP)]
            lhs = jnp.concatenate([avm[p & 255] for p in picks], axis=1)
            rhs = jnp.concatenate([bvm[(p >> 8) & 255] for p in picks], axis=0)
            acc[picks[0] >> 16] += jnp.dot(lhs, rhs, preferred_element_type=jnp.float32)
        return carry

    steps = codes[1, 0] // GROUP
    lax.fori_loop(0, (steps + UNROLL - 1) // UNROLL, body, 0)
    for i in range(CROWS):
        for k in range(CCOLS):
            out[i * edge : (i + 1) * edge, k * edge : (k + 1) * edge] = acc[
                i * CCOLS + k
            ].astype(out.dtype)


def per_device(n_row, n_col, a_blocks, a_rows, b_blocks, b_cols, pair_list, pair_count, row_order):
    a = a_blocks[0, 0]
    b = b_blocks[0, 0]
    n_a, edge, _ = a.shape
    n_b = b.shape[0]
    dt = a.dtype
    dma = pltpu.SemaphoreType.DMA
    most = STOPS * pair_list.shape[-1] + CROWS * CCOLS * GROUP + GROUP * UNROLL
    wide = (most + 127) // 128 * 128
    ar, br, arr, bcr, am, _ = pl.pallas_call(
        functools.partial(gather_kernel, n_row, n_col),
        out_shape=(
            jax.ShapeDtypeStruct((STOPS, n_a, edge, edge), dt),
            jax.ShapeDtypeStruct((STOPS, n_b, edge, edge), dt),
            jax.ShapeDtypeStruct((STOPS, 1, 1, n_a), jnp.int32),
            jax.ShapeDtypeStruct((STOPS, 1, 1, n_b), jnp.int32),
            jax.ShapeDtypeStruct((n_a, edge, edge), dt),
            jax.ShapeDtypeStruct((DETOUR * n_b // CHUNKS, edge, edge), dt),
        ),
        in_specs=[ANY] * 4,
        out_specs=(ANY,) * 6,
        scratch_shapes=[
            dma((4, A_CHUNKS)),
            dma((STOPS, A_CHUNKS)),
            dma((8, CHUNKS)),
            dma((STOPS, CHUNKS)),
            dma((2 * STOPS,)),
            dma((2 * STOPS,)),
            dma((A_CHUNKS + DETOUR,)),
            dma((A_CHUNKS + DETOUR,)),
            dma((DETOUR,)),
        ],
        compiler_params=pltpu.CompilerParams(collective_id=0, has_side_effects=True),
        name="gather",
    )(a, b, a_rows, b_cols)
    return pl.pallas_call(
        functools.partial(multiply_kernel, n_col),
        out_shape=jax.ShapeDtypeStruct((CROWS * edge, CCOLS * edge), dt),
        in_specs=[ANY] * 5 + [VMEM] * 5 + [SMEM] * 2,
        out_specs=pl.BlockSpec(memory_space=pltpu.VMEM),
        scratch_shapes=[
            pltpu.VMEM((STOPS * n_a + 1, edge, edge), dt),
            pltpu.VMEM((STOPS * n_b, edge, edge), dt),
            pltpu.VMEM((CROWS * CCOLS, edge, edge), jnp.float32),
            pltpu.VMEM((8, wide), jnp.int32),
            pltpu.SMEM((8, wide), jnp.int32),
            dma((STOPS,)),
            dma((STOPS,)),
            dma,
        ],
        name="multiply",
    )(a, b, ar, br, am, a_rows, b_cols, arr, bcr, pair_list, pair_count, row_order)


def solution(mesh):
    placed = (
        P("row", "col", None, None, None),
        P("row", "col", None),
        P("row", "col", None, None, None),
        P("row", "col", None),
        P("row", "col", None, None, None),
        P("row", "col", None),
        P("row", None),
    )
    return jax.shard_map(
        functools.partial(per_device, mesh.shape["row"], mesh.shape["col"]),
        mesh=mesh,
        in_specs=placed,
        out_specs=P("row", "col"),
        check_vma=False,
    )
```

```python
import functools

import jax
import jax.numpy as jnp
from jax import lax
from jax.experimental import pallas as pl
from jax.experimental.pallas import tpu as pltpu
from jax.sharding import PartitionSpec as P

CROWS = 4
CCOLS = 8
STOPS = 4
CHUNKS = 8
UNROLL = 64
GROUP = 2
LAG = 6
DETOUR = 2
DETOUR_K = 3
FIRST = 3
A_CHUNKS = 4
ACROSS_AT = 1
ACROSS_BY = 2
MESH = pl.DeviceIdType.MESH
ANY = pl.BlockSpec(memory_space=pl.ANY)
VMEM = pl.BlockSpec(memory_space=pltpu.VMEM)
SMEM = pl.BlockSpec(memory_space=pltpu.SMEM)


def tree(jt, half):
    if jt == 3:
        return (0, ((0, 1), (0, 2), (2, 3))) if half else (2, ((2, 3), (2, 0), (0, 1)))
    if jt == 2:
        return (0, ((0, 3), (0, 1), (1, 2))) if half else (1, ((1, 2), (1, 0), (0, 3)))
    if jt == 1:
        return (2, ((2, 3), (2, 0), (0, 1))) if half else (0, ((0, 1), (0, 2), (2, 3)))
    return (1, ((1, 2), (1, 3), (3, 0))) if half else (0, ((0, 3), (3, 1), (1, 2)))


def plan_of(y, j):
    jt = (j - y) % 4
    landing = tree(jt, j // 2)[0]
    relays = []
    for w in range(STOPS):
        jt = (j + w) % 4
        land, hops = tree(jt, (jt + y) % 4 // 2)
        depth = {land: 0}
        for src, dst in hops:
            depth[dst] = depth[src] + 1
        relays.append((depth[w], w, tuple(dst for src, dst in hops if src == w)))
    return landing, tuple(sorted(relays))


def gather_kernel(
    n_row, n_col, a, b, arow, bcol, ar, br, arr, bcr, am, tb,
    a_ss, a_rs, b_ss, b_rs, m_ss, m_rs, x_ss, x_rs, f_ss,
):
    r = lax.axis_index("row")
    c = lax.axis_index("col")
    j = lax.rem(r, 4)
    y = lax.rem(c, 4)
    mirror = lax.rem(c + 4, n_col)
    partner = n_col - 1 - c
    step = b.shape[0] // CHUNKS
    bar = pltpu.get_barrier_semaphore()

    def rc(src, dst, ss, rs, dev):
        return pltpu.make_async_remote_copy(
            src, dst, ss, rs, device_id=dev, device_id_type=MESH
        )

    def row(d):
        return lax.rem(r + d + n_row, n_row)

    def signal(dev):
        pl.semaphore_signal(bar, 1, device_id=dev, device_id_type=MESH)

    def a_dst(s):
        return lax.rem(c - r - s + 8 * n_col, n_col)

    for d in range(1, n_col):
        signal((r, lax.rem(c + d, n_col)))
    for s in range(STOPS):

        @pl.when(c + s != 0)
        def _():
            signal((lax.rem(r + c + s, n_row), c))
            signal((lax.rem(r - c - s + n_row, n_row), c))

    for d in (1, 2, 3):
        signal((row(d), c))
        signal((row(-d), c))
    far = c >= 4
    detours = (lax.max(c, partner) - 2) // 2
    for w in range(STOPS):

        @pl.when(far)
        def _():
            signal((lax.rem(r + c + w, n_row), partner))

    pl.semaphore_wait(
        bar,
        n_col - 1 + 2 * (STOPS - jnp.where(c == 0, 1, 0)) + 6 + jnp.where(far, 0, STOPS),
    )

    def chunk(k):
        return pl.ds(k * step, step)

    a_step = a.shape[0] // A_CHUNKS

    def a_chunk(q):
        return pl.ds(q * a_step, a_step)

    def across(q):
        return rc(a.at[a_chunk(q)], am.at[a_chunk(q)], x_ss.at[q], x_rs.at[q], (r, mirror))


    def detour_copy(i):
        part = pl.ds(i * step, step)
        return rc(b.at[chunk(DETOUR_K + i)], tb.at[part], x_ss.at[A_CHUNKS + i], x_rs.at[A_CHUNKS + i], (r, partner))

    for i in range(DETOUR):

        @pl.when(far & (i < detours))
        def _():
            detour_copy(i).start()

    for q in range(A_CHUNKS):
        across(q).start()

    def landing_copy(k, w, dev):
        return rc(b.at[chunk(k)], br.at[w, chunk(k)], b_ss.at[0, k], b_rs.at[w, k], dev)

    def landing_of(column):
        jt = lax.rem(j - column + 4, 4)
        found = jnp.int32(0)
        for t in range(4):
            for h in range(2):
                found = jnp.where((jt == t) & (j // 2 == h), tree(t, h)[0], found)
        return found

    landing = landing_of(y)
    partner_landing = landing_of(3 - y)
    own_b = c == 0

    def direct(k):
        return jnp.logical_not(own_b) & (
            jnp.logical_not(far) | (k < DETOUR_K) | (k - DETOUR_K >= detours)
        )

    def send_right(k):
        @pl.when(direct(k))
        def _():
            landing_copy(k, landing, (lax.rem(r - c - landing + n_row, n_row), c)).start()

    for k in range(FIRST):
        send_right(k)

    def far_copy(i):
        k = DETOUR_K + i
        dev = (lax.rem(r - partner - partner_landing + n_row, n_row), partner)
        return rc(
            tb.at[pl.ds(i * step, step)], br.at[partner_landing, chunk(k)],
            f_ss.at[i], b_rs.at[partner_landing, k], dev,
        )

    for s in range(STOPS):

        @pl.when(lax.rem(r + s, n_col) != 0)
        def _():
            rc(arow, arr.at[s], m_ss.at[s], m_rs.at[s], (r, a_dst(s))).start()

        @pl.when(c + s != 0)
        def _():
            rc(
                bcol, bcr.at[s], m_ss.at[STOPS + s], m_rs.at[STOPS + s],
                (lax.rem(r - c - s + n_row, n_row), c),
            ).start()

    def ring_copy(d, src, q):
        to = c - y + lax.rem(y + d, 4)
        stop = lax.rem(c - to - r + 8 * n_col, n_col)
        own = stop < 4
        stop = lax.rem(stop, 4)
        return own, rc(
            src.at[a_chunk(q)], ar.at[stop, a_chunk(q)], a_ss.at[d, q], a_rs.at[stop, q], (r, to)
        )

    for d in (1, 3, 2):
        for q in range(A_CHUNKS):
            own, copy = ring_copy(d, a, q)

            @pl.when(own)
            def _():
                copy.start()

    for i in range(DETOUR):

        @pl.when(jnp.logical_not(far) & (i < detours))
        def _():
            detour_copy(i).wait_recv()
            far_copy(i).start()

        if i == 0:
            for k in range(FIRST, CHUNKS):
                send_right(k)

    def wait_recv(w, k):
        rc(br.at[w, chunk(k)], br.at[w, chunk(k)], b_ss.at[0, k], b_rs.at[w, k], (r, c)).wait_recv()

    def relay_copy(w, to, k, slot, own):
        src = b.at[chunk(k)] if own else br.at[w, chunk(k)]
        return rc(src, br.at[to, chunk(k)], b_ss.at[slot, k], b_rs.at[to, k], (row(w - to), c))

    def run(relays, own):
        slots = {}
        for _, w, dests in relays:
            for to in dests:
                slots[w, to] = len(slots) + 1
        events = sorted(
            (k + LAG * depth, depth, k, w, dests)
            for depth, w, dests in relays
            for k in range(CHUNKS)
        )
        def relay_left(q):
            across(q).wait_recv()
            for d in (1, 3, 2):
                first, copy = ring_copy(d, am, q)

                @pl.when(jnp.logical_not(first))
                def _():
                    copy.start()

        extra = []
        for q in range(A_CHUNKS):
            extra.append((ACROSS_AT + q * ACROSS_BY, functools.partial(relay_left, q)))
        for at in range(max(len(events), 1 + max(e[0] for e in extra))):
            if at < len(events):
                _, depth, k, w, dests = events[at]
                mine = own and w == 0
                if not mine:
                    wait_recv(w, k)
                for to in dests:
                    relay_copy(w, to, k, slots[w, to], mine).start()
            for when, action in extra:
                if when == at:
                    action()

        for k in range(CHUNKS):
            slot = 1
            for _, w, dests in relays:
                for to in dests:
                    relay_copy(w, to, k, slot, own and w == 0).wait_send()
                    slot += 1

    for jj in range(4):
        for yy in range(4):
            for own in (False, True) if yy == 0 else (False,):
                here = (j == jj) & (y == yy)
                if yy == 0:
                    here = here & (own_b if own else jnp.logical_not(own_b))

                @pl.when(here)
                def _():
                    run(plan_of(yy, jj)[1], own)

    for k in range(CHUNKS):

        @pl.when(direct(k))
        def _():
            landing_copy(k, 0, (r, c)).wait_send()

    for i in range(DETOUR):

        @pl.when(far & (i < detours))
        def _():
            detour_copy(i).wait_send()

        @pl.when(jnp.logical_not(far) & (i < detours))
        def _():
            far_copy(i).wait_send()

    for q in range(A_CHUNKS):
        across(q).wait_send()
        for d in (1, 3, 2):
            ring_copy(d, a, q)[1].wait_send()
    for s in range(STOPS):

        @pl.when(lax.rem(r + s, 4) != 0)
        def _():
            for q in range(A_CHUNKS):
                part = ar.at[s, a_chunk(q)]
                rc(part, part, a_ss.at[1, q], a_rs.at[s, q], (r, c)).wait_recv()

        @pl.when(lax.rem(r + s, n_col) != 0)
        def _():
            rc(arow, arr.at[s], m_ss.at[s], m_rs.at[s], (r, c)).wait()

        @pl.when(c + s != 0)
        def _():
            rc(bcol, bcr.at[s], m_ss.at[STOPS + s], m_rs.at[STOPS + s], (r, c)).wait()


def multiply_kernel(
    n_col, a, b, ar, br, am, arow, bcol, arr, bcr, pairs, count, order, out,
    avm, bvm, acc, codes_v, codes, a_sem, b_sem, c_sem,
):
    r = lax.axis_index("row")
    c = lax.axis_index("col")
    n_a = a.shape[0]
    n_b = b.shape[0]
    n_pairs = pairs.shape[-1]
    edge = acc.shape[1]
    n_t = CROWS * CCOLS

    for s in range(STOPS):
        a_to = avm.at[pl.ds(1 + s * n_a, n_a)]

        @pl.when(lax.rem(r + s, n_col) == 0)
        def _():
            pltpu.make_async_copy(a, a_to, a_sem.at[s]).start()

        @pl.when(lax.rem(r + s, n_col) == 4)
        def _():
            pltpu.make_async_copy(am, a_to, a_sem.at[s]).start()

        @pl.when(lax.rem(r + s, 4) != 0)
        def _():
            pltpu.make_async_copy(ar.at[s], a_to, a_sem.at[s]).start()

        if s == 0:

            @pl.when(c == 0)
            def _():
                pltpu.make_async_copy(b, bvm.at[pl.ds(s * n_b, n_b)], b_sem.at[s]).start()

            @pl.when(c != 0)
            def _():
                pltpu.make_async_copy(br.at[s], bvm.at[pl.ds(s * n_b, n_b)], b_sem.at[s]).start()
        else:
            pltpu.make_async_copy(br.at[s], bvm.at[pl.ds(s * n_b, n_b)], b_sem.at[s]).start()
    avm[0] = jnp.zeros((edge, edge), avm.dtype)

    i32 = jnp.int32
    lane = lax.broadcasted_iota(i32, (1, n_pairs), 1)
    wide = codes_v.shape[1]
    stops = []
    for s in range(STOPS):
        rows = jnp.where(lax.rem(r + s, n_col) == 0, arow[0], arr[s, 0])
        cols = jnp.where(c + s == 0, bcol[0], bcr[s, 0])
        placed = jnp.zeros_like(rows)
        for i in range(CROWS):
            placed = placed + jnp.where(rows == i, order[0, i], 0)
        left = pairs[0, 0, s, 0:1, :]
        right = pairs[0, 0, s, 1:2, :]
        target = jnp.zeros_like(left)
        for l in range(n_a):
            target = target + jnp.where(left == l, placed[:, l : l + 1] * CCOLS, 0)
        for k in range(n_b):
            target = target + jnp.where(right == k, cols[:, k : k + 1], 0)
        live = lane < count[0, 0, s]
        stops.append(jnp.where(live, target, n_t))
        stops.append(target * 65536 + (right + s * n_b) * 256 + left + s * n_a + 1)
    table = jnp.concatenate(stops, axis=0).T
    here = lax.broadcasted_iota(i32, (n_pairs, n_pairs), 0)
    there = lax.broadcasted_iota(i32, (n_pairs, n_pairs), 1)
    earlier = there < here
    t_lane = lax.broadcasted_iota(i32, (n_pairs, 128), 1)
    slot = lax.broadcasted_iota(i32, (n_pairs, wide), 1)
    listed = jnp.zeros((1, wide), i32)
    total = jnp.zeros((1, 128), i32)
    earlier_stops = []
    for s in range(STOPS):
        earlier_stops.append(total)
        t_col = table[:, 2 * s : 2 * s + 1]
        total = total + jnp.sum(jnp.where(t_col == t_lane, 1, 0), axis=0, keepdims=True)
    held = jnp.where(t_lane[0:1] < n_t, (total + GROUP - 1) // GROUP * GROUP, 0)
    for s in range(STOPS):
        t_row = stops[2 * s]
        t_col = table[:, 2 * s : 2 * s + 1]
        code = table[:, 2 * s + 1 : 2 * s + 2]
        rank = jnp.sum(jnp.where((t_row == t_col) & earlier, 1, 0), axis=1, keepdims=True)
        ahead = jnp.where(t_lane < t_col, held, jnp.where(t_lane == t_col, earlier_stops[s], 0))
        before = jnp.sum(ahead, axis=1, keepdims=True)
        place = jnp.where(t_col < n_t, before + rank, wide)
        listed = listed + jnp.sum(jnp.where(place == slot, code, 0), axis=0, keepdims=True)
    codes_v[0:1, :] = listed
    codes_v[1:2, :] = jnp.broadcast_to(jnp.sum(held, axis=1, keepdims=True), (1, wide))

    acc[...] = jnp.zeros_like(acc)
    listing = pltpu.make_async_copy(codes_v, codes, c_sem)
    listing.start()
    listing.wait()
    for s in range(STOPS):
        pltpu.make_async_copy(ar.at[s], avm.at[pl.ds(1 + s * n_a, n_a)], a_sem.at[s]).wait()
        pltpu.make_async_copy(br.at[s], bvm.at[pl.ds(s * n_b, n_b)], b_sem.at[s]).wait()

    def body(t, carry):
        for u in range(UNROLL):
            at = (t * UNROLL + u) * GROUP
            picks = [codes[0, at + g] for g in range(GROUP)]
            lhs = jnp.concatenate([avm[p & 255] for p in picks], axis=1)
            rhs = jnp.concatenate([bvm[(p >> 8) & 255] for p in picks], axis=0)
            acc[picks[0] >> 16] += jnp.dot(lhs, rhs, preferred_element_type=jnp.float32)
        return carry

    steps = codes[1, 0] // GROUP
    lax.fori_loop(0, (steps + UNROLL - 1) // UNROLL, body, 0)
    for i in range(CROWS):
        for k in range(CCOLS):
            out[i * edge : (i + 1) * edge, k * edge : (k + 1) * edge] = acc[
                i * CCOLS + k
            ].astype(out.dtype)


def per_device(n_row, n_col, a_blocks, a_rows, b_blocks, b_cols, pair_list, pair_count, row_order):
    a = a_blocks[0, 0]
    b = b_blocks[0, 0]
    n_a, edge, _ = a.shape
    n_b = b.shape[0]
    dt = a.dtype
    dma = pltpu.SemaphoreType.DMA
    most = STOPS * pair_list.shape[-1] + CROWS * CCOLS * GROUP + GROUP * UNROLL
    wide = (most + 127) // 128 * 128
    ar, br, arr, bcr, am, _ = pl.pallas_call(
        functools.partial(gather_kernel, n_row, n_col),
        out_shape=(
            jax.ShapeDtypeStruct((STOPS, n_a, edge, edge), dt),
            jax.ShapeDtypeStruct((STOPS, n_b, edge, edge), dt),
            jax.ShapeDtypeStruct((STOPS, 1, 1, n_a), jnp.int32),
            jax.ShapeDtypeStruct((STOPS, 1, 1, n_b), jnp.int32),
            jax.ShapeDtypeStruct((n_a, edge, edge), dt),
            jax.ShapeDtypeStruct((DETOUR * n_b // CHUNKS, edge, edge), dt),
        ),
        in_specs=[ANY] * 4,
        out_specs=(ANY,) * 6,
        scratch_shapes=[
            dma((4, A_CHUNKS)),
            dma((STOPS, A_CHUNKS)),
            dma((8, CHUNKS)),
            dma((STOPS, CHUNKS)),
            dma((2 * STOPS,)),
            dma((2 * STOPS,)),
            dma((A_CHUNKS + DETOUR,)),
            dma((A_CHUNKS + DETOUR,)),
            dma((DETOUR,)),
        ],
        compiler_params=pltpu.CompilerParams(collective_id=0, has_side_effects=True),
        name="gather",
    )(a, b, a_rows, b_cols)
    return pl.pallas_call(
        functools.partial(multiply_kernel, n_col),
        out_shape=jax.ShapeDtypeStruct((CROWS * edge, CCOLS * edge), dt),
        in_specs=[ANY] * 5 + [VMEM] * 5 + [SMEM] * 2,
        out_specs=pl.BlockSpec(memory_space=pltpu.VMEM),
        scratch_shapes=[
            pltpu.VMEM((STOPS * n_a + 1, edge, edge), dt),
            pltpu.VMEM((STOPS * n_b, edge, edge), dt),
            pltpu.VMEM((CROWS * CCOLS, edge, edge), jnp.float32),
            pltpu.VMEM((8, wide), jnp.int32),
            pltpu.SMEM((8, wide), jnp.int32),
            dma((STOPS,)),
            dma((STOPS,)),
            dma,
        ],
        name="multiply",
    )(a, b, ar, br, am, a_rows, b_cols, arr, bcr, pair_list, pair_count, row_order)


def solution(mesh):
    placed = (
        P("row", "col", None, None, None),
        P("row", "col", None),
        P("row", "col", None, None, None),
        P("row", "col", None),
        P("row", "col", None, None, None),
        P("row", "col", None),
        P("row", None),
    )
    return jax.shard_map(
        functools.partial(per_device, mesh.shape["row"], mesh.shape["col"]),
        mesh=mesh,
        in_specs=placed,
        out_specs=P("row", "col"),
        check_vma=False,
    )
```
